32 devices in a mesh: pipe: 2 (over core), dp: 4 (over z), tensor: 4 (over y, x).
Axes of the slice: x: 2, y: 2, z: 4, core: 2. Of those that a mesh axis runs over, the one named last changes fastest.
Arguments:
- tokens_in: bfloat16 [2, 1024, 2048], P(None, ('dp', 'tensor')), may hold values from -6 to 6
- out_grad: bfloat16 [2, 1024, 2048], P(None, ('dp', 'tensor')), may hold values from -6 to 6
- seq_lengths: int32 [2, 4, 8], P(None, 'dp'), may hold values from 0 to 256, as said below
- norm_gains: bfloat16 [2, 2, 2048], P('pipe', None, 'dp'), may hold values from 0.5 to 1.5
- norm_shifts: bfloat16 [2, 2, 2048], P('pipe', None, 'dp'), may hold values from -2.5 to 2.5
- w_qkv: bfloat16 [2, 2048, 3, 2048], P('pipe', 'dp', None, 'tensor'), may hold values from -0.125 to 0.125
- b_qkv: bfloat16 [2, 3, 32, 64], P('pipe', None, 'tensor', 'dp'), may hold values from -2 to 2
- w_out: bfloat16 [2, 2048, 2048], P('pipe', 'tensor', 'dp'), may hold values from -0.5 to 0.5
- w_gate_up: bfloat16 [2, 2048, 2, 5632], P('pipe', 'dp', None, 'tensor'), may hold values from -0.125 to 0.125
- w_down: bfloat16 [2, 5632, 2048], P('pipe', 'tensor', 'dp'), may hold values from -0.078125 to 0.078125
Outputs:
- section_outs: bfloat16 [2, 2, 1024, 2048], P('pipe', None, ('dp', 'tensor'))
- input_grads: bfloat16 [2, 2, 1024, 2048], P('pipe', None, ('dp', 'tensor'))
- grad_gains: float32 [2, 2, 2048], P('pipe', None, 'dp')
- grad_shifts: float32 [2, 2, 2048], P('pipe', None, 'dp')
- grad_qkv: float32 [2, 2048, 3, 2048], P('pipe', 'dp', None, 'tensor')
- grad_bias: float32 [2, 3, 32, 64], P('pipe', None, 'tensor', 'dp')
- grad_out: float32 [2, 2048, 2048], P('pipe', 'tensor', 'dp')
- grad_gate_up: float32 [2, 2048, 2, 5632], P('pipe', 'dp', None, 'tensor')
- grad_down: float32 [2, 5632, 2048], P('pipe', 'tensor', 'dp')
The draws below stay inside these ranges and needn't reach their ends.
Inputs may be any that keep to these rules, and one draw needn't show every extreme that they name: `seq_lengths`: each slot's lengths sum to at most 256; in every draw some slot holds one sequence of all 256 positions and empty places after it.
All inputs are finite; a program needn't handle non-finite values.
Results may differ from the reference program's by a relative error of at most 0.017.
Values may be sent and summed in bfloat16 or wider, within the bound.
No kernel may reach another device: no remote copies, remote signals or barrier semaphores. Data moves between devices by JAX's collectives and lax.ppermute only.
A program may use at most 192 MiB of HBM per device.

```python
import math
import jax
import jax.numpy as jnp
from jax import lax

HEADS = 32
HD = 64
FF = 5632
D = 2048
SLOT = 256
MB = 2
SEQS = 8
LAYERS = 2
TOKENS = 1024
N_DP = 4


def draw_seq_lengths(key, part):
    slot_count = MB * N_DP
    load_key, cut_key, full_key = jax.random.split(key, 3)
    slot_loads = jax.random.randint(load_key, (slot_count, 1), SLOT // 4, SLOT + 1)
    cut_points = jax.random.randint(cut_key, (slot_count, SEQS - 1), 0, slot_loads + 1)
    cut_points = jnp.sort(cut_points, axis=1)
    boundaries = jnp.concatenate([jnp.zeros((slot_count, 1), jnp.int32), cut_points.astype(jnp.int32), slot_loads.astype(jnp.int32)], axis=1)
    lengths = boundaries[:, 1:] - boundaries[:, :-1]
    full_slot = jax.random.randint(full_key, (), 0, slot_count)
    single = jnp.zeros((SEQS,), jnp.int32).at[0].set(SLOT)
    lengths = jnp.where((jnp.arange(slot_count) == full_slot)[:, None], single[None, :], lengths)
    return lengths.reshape(MB, N_DP, SEQS).astype(jnp.int32)


def draw_b_qkv(key, part):
    base_key = jax.random.fold_in(key, 0)
    biases = jnp.clip(0.5 * jax.random.normal(base_key, (LAYERS, 3, HEADS, HD), jnp.float32), -2.0, 2.0)
    return biases.astype(jnp.bfloat16)


def steps_of(rng, dims, cuts, least, high):
    loudness = 1.0
    for position, parts in cuts:
        steps = jax.random.uniform(jax.random.fold_in(jax.random.fold_in(rng, 6), position), (parts,), jnp.float32, least / len(cuts), high / len(cuts))
        loudness = loudness * jnp.repeat(jnp.exp(steps), dims[position] // parts).reshape((-1,) + (1,) * (len(dims) - 1 - position))
    return loudness


def scatter_about(rng, extent, width, bound, cuts=(), kind=jnp.bfloat16):
    entries = width * jax.random.normal(rng, extent, jnp.float32)
    if cuts:
        entries = entries * steps_of(rng, extent, cuts, -0.22, 0.18)
    return jnp.clip(entries, -bound, bound).astype(kind)


def setup_inputs(seed: int = 0) -> dict:
    keys = jax.random.split(jax.random.key(seed), 11)
    return {
        "tokens_in": scatter_about(keys[0], (MB, TOKENS, D), 1.0, 6.0, ((1, 16),)),
        "out_grad": scatter_about(keys[1], (MB, TOKENS, D), 1.0, 6.0, ((1, 16),)),
        "seq_lengths": draw_seq_lengths(jax.random.fold_in(keys[10], 71), 0),
        "norm_gains": jnp.clip(1.0 + 0.1 * jax.random.normal(keys[3], (LAYERS, 2, D), jnp.float32), 0.5, 1.5).astype(jnp.bfloat16),
        "norm_shifts": scatter_about(keys[4], (LAYERS, 2, D), 0.3, 2.5, ((0, 2), (2, 4))),
        "w_qkv": scatter_about(keys[5], (LAYERS, D, 3, D), D ** -0.5, 0.125, ((0, 2), (1, 4), (3, 4))),
        "b_qkv": draw_b_qkv(jax.random.fold_in(keys[10], 71), 0),
        "w_out": scatter_about(keys[7], (LAYERS, D, D), (D // 16) ** -0.5, 0.5, ((0, 2), (1, 4), (2, 4))),
        "w_gate_up": scatter_about(keys[8], (LAYERS, D, 2, FF), D ** -0.5, 0.125, ((0, 2), (1, 4), (3, 4))),
        "w_down": scatter_about(keys[9], (LAYERS, FF, D), FF ** -0.5, 0.078125, ((0, 2), (1, 4), (2, 4))),
    }


@jax.custom_vjp
def low(v):
    return lax.optimization_barrier(v.astype(jnp.bfloat16)).astype(jnp.float32)

@jax.custom_vjp
def low_back(v):
    return v

def low_keep(v):
    return (low(v), None)

def low_pass(kept, grad):
    return (grad,)

def back_keep(v):
    return (v, None)

def back_low(kept, grad):
    return (low(grad),)
low.defvjp(low_keep, low_pass)
low_back.defvjp(back_keep, back_low)
eps_norm = 1e-05
masked_score = -1e+30
rope_base = 10000.0
highest = lax.Precision.HIGHEST

def slot_layout(lengths, slot_rows):
    seq_count = lengths.shape[0]
    seq_ends = jnp.cumsum(lengths).astype(jnp.int32)
    starts = (seq_ends - lengths).astype(jnp.int32)
    places = jnp.arange(slot_rows, dtype=jnp.int32)
    segment = lax.optimization_barrier(jnp.sum((seq_ends[None, :] <= places[:, None]).astype(jnp.int32), axis=1)).astype(jnp.int32)
    member_of = segment[:, None] == jnp.arange(seq_count, dtype=jnp.int32)[None, :]
    opening = lax.optimization_barrier(jnp.sum(jnp.where(member_of, starts[None, :], 0), axis=1)).astype(jnp.int32)
    positions = (places - opening).astype(jnp.int32)
    return (segment, positions, (segment < seq_count).astype(jnp.float32))

def rotary_tables(positions, head_dim):
    half_dim = head_dim // 8
    frequency = rope_base ** (-jnp.arange(half_dim, dtype=jnp.float32) / half_dim)
    angles = positions.astype(jnp.float32)[:, None] * frequency[None, :]
    return (jnp.cos(angles)[:, None, :], jnp.sin(angles)[:, None, :])

def rotate(heads_in, cos_table, sin_table, direction):
    half_dim = cos_table.shape[-1]
    leading = heads_in[..., :half_dim]
    trailing = heads_in[..., half_dim:2 * half_dim]
    remainder = heads_in[..., 2 * half_dim:]
    return jnp.concatenate([leading * cos_table - direction * trailing * sin_table, trailing * cos_table + direction * leading * sin_table, remainder], axis=-1)

def layer_norm(section_rows, norm_gain, norm_shift):
    row_mean = lax.optimization_barrier(jnp.mean(section_rows, axis=-1, keepdims=True))
    centred = section_rows - row_mean
    spread = lax.optimization_barrier(jnp.mean(centred * centred, axis=-1, keepdims=True))
    return centred * lax.rsqrt(spread + eps_norm) * norm_gain + norm_shift

def layer(section_rows, params, layouts):
    norm_gain, norm_shift, qkv_weight, qkv_bias, out_weight, gu_weight, down_weight = params
    segment, positions, valid_rows = layouts
    score_scale = 1.0 / math.sqrt(HD)
    normed_one = low(layer_norm(section_rows, norm_gain[0], norm_shift[0]))
    projected = jnp.einsum('nsd,dkc->nskc', normed_one, qkv_weight, precision=highest) + qkv_bias.reshape(3, D)
    projected = low_back(projected)

    def attend(pieces):
        slot_projected, slot_segment, slot_positions = pieces
        head_parts = slot_projected.reshape(SLOT, 3, HEADS, HD)
        cos_table, sin_table = rotary_tables(slot_positions, HD)
        queries = low(rotate(head_parts[:, 0], cos_table, sin_table, 1.0))
        key_rows = low(rotate(head_parts[:, 1], cos_table, sin_table, 1.0))
        value_rows = low(head_parts[:, 2])
        scores = low_back(jnp.einsum('qhd,khd->hqk', queries, key_rows, precision=highest) * score_scale)
        places = jnp.arange(SLOT, dtype=jnp.int32)
        allowed = (slot_segment[:, None] == slot_segment[None, :]) & (places[:, None] >= places[None, :])
        scores = jnp.where(allowed[None], scores, masked_score)
        attention = low(jax.nn.softmax(scores, axis=-1))
        mixed_heads = jnp.einsum('hqk,khd->qhd', attention, value_rows, precision=highest)
        return low(low_back(mixed_heads.reshape(SLOT, D)))
    attended = lax.map(jax.checkpoint(attend), (projected, segment, positions))
    branch = low_back(jnp.einsum('nsc,cd->nsd', attended, out_weight, precision=highest))
    middle = section_rows + branch
    normed_two = low(layer_norm(middle, norm_gain[1], norm_shift[1]))
    gate_up = low_back(jnp.einsum('nsd,dkf->nskf', normed_two, gu_weight, precision=highest))
    hidden = low(jax.nn.silu(gate_up[:, :, 0]) * gate_up[:, :, 1])
    down_branch = low_back(jnp.einsum('nsf,fd->nsd', hidden, down_weight, precision=highest))
    return (middle + down_branch) * valid_rows[..., None]

def reference(tokens_in, out_grad, seq_lengths, norm_gains, norm_shifts, w_qkv, b_qkv, w_out, w_gate_up, w_down):
    slot_count = MB * N_DP
    layouts = jax.vmap(lambda lengths: slot_layout(lengths, SLOT))(seq_lengths.reshape(slot_count, SEQS))

    def layer_params(layer_index):
        return tuple((weight.astype(jnp.float32)[layer_index] for weight in (norm_gains, norm_shifts, w_qkv, b_qkv, w_out, w_gate_up, w_down)))

    def section_apply(section_rows, params):
        return layer(section_rows, params, layouts)
    first_rows = tokens_in.astype(jnp.float32).reshape(slot_count, SLOT, D)
    first_out, first_pull = jax.vjp(section_apply, first_rows, layer_params(0))
    passed = first_out.astype(jnp.bfloat16)
    second_out, second_pull = jax.vjp(section_apply, passed.astype(jnp.float32), layer_params(1))
    grad_passed, second_grads = second_pull(out_grad.astype(jnp.float32).reshape(slot_count, SLOT, D))
    grad_passed = grad_passed.astype(jnp.bfloat16)
    grad_tokens, first_grads = first_pull(grad_passed.astype(jnp.float32))
    section_outs = jnp.stack([passed, second_out.astype(jnp.bfloat16)]).reshape(LAYERS, MB, TOKENS, D)
    input_grads = jnp.stack([grad_tokens.astype(jnp.bfloat16), grad_passed]).reshape(LAYERS, MB, TOKENS, D)
    weight_grads = tuple((jnp.stack([early_grad, late_grad]) for early_grad, late_grad in zip(first_grads, second_grads)))
    return (section_outs, input_grads, weight_grads[0], weight_grads[1], weight_grads[2], weight_grads[3], weight_grads[4], weight_grads[5], weight_grads[6])
```

```python
import math

import jax
import jax.numpy as jnp
from jax import lax
from jax.sharding import PartitionSpec as P


eps_norm = 1e-05
masked_score = -1e30
rope_base = 10000.0
f32 = jnp.float32
bf16 = jnp.bfloat16


def pick(array, index):
    return lax.dynamic_index_in_dim(array, index, 0, keepdims=False)


def after(array, other):
    return lax.optimization_barrier((array, other))[0]


def dot_nt(a, b):
    return lax.dot_general(a, b, (((1,), (1,)), ((), ())), preferred_element_type=f32)


def dot_nn(a, b):
    return lax.dot_general(a, b, (((1,), (0,)), ((), ())), preferred_element_type=f32)


def dot_tn(a, b):
    return lax.dot_general(a, b, (((0,), (0,)), ((), ())), preferred_element_type=f32)


class Place:
    def __init__(self):
        self.nd = lax.axis_size("dp")
        self.nt = lax.axis_size("tensor")
        self.tp = self.nt
        self.hi = self.nd // self.tp
        self.c = lax.axis_index("pipe")
        self.g = lax.axis_index("dp")
        self.j = lax.axis_index("tensor")
        self.lo = self.g % self.tp

    def swap(self, x):
        return lax.ppermute(x, "pipe", [(0, 1), (1, 0)])

    def lo_xor(self, x, b):
        return lax.ppermute(
            x, "dp", [(h * self.tp + i, h * self.tp + (i ^ b)) for h in range(self.hi) for i in range(self.tp)]
        )

    def lo_shift(self, x, s):
        tp = self.tp
        return lax.ppermute(
            x, "dp", [(h * tp + i, h * tp + (i + s) % tp) for h in range(self.hi) for i in range(tp)]
        )

    def t_xor(self, x, b):
        return lax.ppermute(x, "tensor", [(i, i ^ b) for i in range(self.nt)])

    def turn(self, x):
        tp, nt = self.tp, self.nt
        pairs = [
            ((h * tp + l) * nt + t, (h * tp + t) * nt + l)
            for h in range(self.hi)
            for l in range(tp)
            for t in range(nt)
        ]
        return lax.ppermute(x, ("dp", "tensor"), pairs)

    def hi_groups(self):
        return [[h * self.tp + i for h in range(self.hi)] for i in range(self.tp)]

    def e_order(self):
        order = [0]
        bit = self.tp // 2
        while bit:
            order = order + [e ^ bit for e in order]
            bit //= 2
        return order

    def gather_rows(self, x):
        blocks = [x]
        bit = self.tp // 2
        while bit:
            blocks = blocks + [self.lo_xor(b, bit) for b in blocks]
            bit //= 2
        mine = jnp.concatenate(blocks, axis=0)
        return [mine, self.swap(mine)]

    def scatter_rows(self, own, other_low):
        total = own + self.swap(other_low).astype(f32)
        bit = 1
        while bit < self.tp:
            half = total.shape[0] // 2
            got = self.lo_xor(total[half:].astype(bf16), bit)
            total = total[:half] + got.astype(f32)
            bit *= 2
        return total

    def weights_in(self, pack):
        slots = [pick(pack, self.lo)]
        for s in range(1, self.tp):
            slots.append(self.lo_shift(pick(pack, (self.lo + s) % self.tp), s))
        stacked = jnp.stack(slots)
        whole = jnp.concatenate([pick(stacked, (self.lo - k) % self.tp) for k in range(self.tp)], axis=1)
        if self.hi > 1:
            every = lax.all_gather(whole, "dp", axis_index_groups=self.hi_groups())
            whole = jnp.concatenate([every[h] for h in range(self.hi)], axis=1)
        return [whole] + [self.t_xor(whole, e) for e in range(1, self.nt)]

    def grads_out(self, pieces):
        total = pieces[0].astype(f32)
        for e in range(1, self.nt):
            total = total + self.t_xor(pieces[e], e).astype(f32)
        if self.hi > 1:
            rows = total.shape[0]
            total = lax.psum_scatter(
                total.reshape(rows, self.hi, -1),
                "dp",
                scatter_dimension=1,
                axis_index_groups=self.hi_groups(),
                tiled=False,
            )
        total = total.astype(bf16)
        width = total.shape[1] // self.tp

        def chunk(k):
            return lax.dynamic_slice_in_dim(total, k * width, width, 1)

        slots = [chunk(self.lo)]
        for s in range(1, self.tp):
            slots.append(self.lo_shift(chunk((self.lo + s) % self.tp), s))
        stacked = jnp.stack(slots)
        return jnp.stack([pick(stacked, (self.lo - k) % self.tp) for k in range(self.tp)])

    def all_dp(self, x):
        slots = [x]
        for s in range(1, self.nd):
            slots.append(lax.ppermute(x, "dp", [(i, (i + s) % self.nd) for i in range(self.nd)]))
        stacked = jnp.stack(slots)
        return jnp.stack([pick(stacked, (self.g - k) % self.nd) for k in range(self.nd)])


def norm_forward(rows, gain, shift):
    row_mean = jnp.mean(rows, axis=-1, keepdims=True)
    centred = rows - row_mean
    inverse = lax.rsqrt(jnp.mean(centred * centred, axis=-1, keepdims=True) + eps_norm)
    unit = centred * inverse
    return (unit * gain + shift).astype(bf16), unit, inverse


def norm_backward(grad_normed, unit, inverse, gain):
    grad_gain = jnp.sum(grad_normed * unit, axis=0)
    grad_shift = jnp.sum(grad_normed, axis=0)
    grad_unit = grad_normed * gain
    grad_rows = inverse * (
        grad_unit
        - jnp.mean(grad_unit, axis=-1, keepdims=True)
        - unit * jnp.mean(grad_unit * unit, axis=-1, keepdims=True)
    )
    return grad_rows, grad_gain, grad_shift


def rotate(rows, tables, direction):
    cos_table, sin_low, sin_high, half = tables
    back = jnp.roll(rows, -half, axis=1)
    ahead = jnp.roll(rows, half, axis=1)
    return rows * cos_table + direction * (back * sin_low + ahead * sin_high)


def slot_tables(lengths, places, heads, head_dim):
    seq_count = lengths.shape[0]
    ends = jnp.cumsum(lengths)
    starts = ends - lengths
    segment = jnp.sum((ends[None, :] <= places[:, None]).astype(jnp.int32), axis=1)
    member = segment[:, None] == jnp.arange(seq_count, dtype=jnp.int32)[None, :]
    opening = jnp.sum(jnp.where(member, starts[None, :], 0), axis=1)
    positions = places - opening
    valid = (segment < seq_count).astype(f32)
    half = head_dim // 8
    frequency = rope_base ** (-jnp.arange(half, dtype=f32) / half)
    angles = positions.astype(f32)[:, None] * frequency[None, :]
    cos, sin = jnp.cos(angles), jnp.sin(angles)
    rest = head_dim - 2 * half
    rows = places.shape[0]
    ones = jnp.ones((rows, rest), f32)
    zero_half = jnp.zeros((rows, half), f32)
    zeros = jnp.zeros((rows, rest), f32)
    cos_table = jnp.tile(jnp.concatenate([cos, cos, ones], axis=1), (1, heads))
    sin_low = jnp.tile(jnp.concatenate([-sin, zero_half, zeros], axis=1), (1, heads))
    sin_high = jnp.tile(jnp.concatenate([zero_half, sin, zeros], axis=1), (1, heads))
    cos_table, sin_low, sin_high = lax.optimization_barrier((cos_table, sin_low, sin_high))
    allowed = (segment[:, None] == segment[None, :]) & (places[:, None] >= places[None, :])
    return valid, allowed, (cos_table, sin_low, sin_high, half)


def heads_of(rows, heads):
    return rows.reshape(rows.shape[0], heads, -1)


def scores_of(queries, keys, allowed, score_scale):
    scores = jnp.einsum("qhd,khd->hqk", queries, keys, preferred_element_type=f32) * score_scale
    return jnp.where(allowed[None], scores, masked_score)


def attend(projected, tables, allowed, heads, score_scale):
    width = projected.shape[1] // 3
    queries = heads_of(rotate(projected[:, :width], tables, 1.0).astype(bf16), heads)
    keys = heads_of(rotate(projected[:, width : 2 * width], tables, 1.0).astype(bf16), heads)
    values = heads_of(projected[:, 2 * width :].astype(bf16), heads)
    scores = scores_of(queries, keys, allowed, score_scale)
    top = jnp.max(scores, axis=-1, keepdims=True)
    exponent = jnp.exp(scores - top)
    total = jnp.sum(exponent, axis=-1, keepdims=True)
    log_total = top + jnp.log(total)
    attention = (exponent / total).astype(bf16)
    mixed = jnp.einsum("hqk,khd->qhd", attention, values, preferred_element_type=f32)
    attended = mixed.reshape(projected.shape[0], width).astype(bf16)
    return attended, (queries, keys, values, log_total)


def attend_back(grad_attended, kept, tables, allowed, heads, score_scale):
    queries, keys, values, log_total = kept
    grad_attended = heads_of(grad_attended, heads)
    attention = jnp.exp(scores_of(queries, keys, allowed, score_scale) - log_total)
    grad_values = jnp.einsum(
        "hqk,qhd->khd", attention.astype(bf16), grad_attended, preferred_element_type=f32
    )
    grad_weights = jnp.einsum("qhd,khd->hqk", grad_attended, values, preferred_element_type=f32)
    inner = jnp.sum(attention * grad_weights, axis=-1, keepdims=True)
    grad_scores = (attention * (grad_weights - inner)).astype(bf16)
    grad_queries = jnp.einsum("hqk,khd->qhd", grad_scores, keys, preferred_element_type=f32) * score_scale
    grad_keys = jnp.einsum("hqk,qhd->khd", grad_scores, queries, preferred_element_type=f32) * score_scale
    rows = grad_queries.shape[0]
    grad_queries = rotate(grad_queries.reshape(rows, -1), tables, -1.0)
    grad_keys = rotate(grad_keys.reshape(rows, -1), tables, -1.0)
    return jnp.concatenate(
        [grad_queries.astype(bf16), grad_keys.astype(bf16), grad_values.reshape(rows, -1).astype(bf16)], axis=1
    )


def on_device(
    tokens_in, out_grad, seq_lengths, norm_gains, norm_shifts, w_qkv, b_qkv, w_out, w_gate_up, w_down
):
    at = Place()
    c, lo, tp, nt, nd = at.c, at.lo, at.tp, at.nt, at.nd
    first_core = c == 0
    micro, rows_local, width = tokens_in.shape
    part = w_qkv.shape[1]
    heads_j = b_qkv.shape[2]
    head_dim = b_qkv.shape[3] * nd
    per = heads_j // (2 * tp)
    heads = nt * per
    head_rows = per * head_dim
    ff_rows = w_down.shape[1] // (2 * tp)
    score_scale = 1.0 / math.sqrt(head_dim)

    own_tokens = at.turn(pick(tokens_in, c))
    own_grad = at.turn(pick(out_grad, c))
    lengths = at.turn(seq_lengths[:, 0])

    qkv_t = w_qkv[0].reshape(part, 3 * heads_j * head_dim).T.reshape(3, tp, 2, head_rows, part)
    attn_pack = jnp.concatenate(
        [qkv_t.transpose(1, 2, 0, 3, 4).reshape(tp, 2, 3 * head_rows, part), w_out[0].reshape(tp, 2, head_rows, part)],
        axis=2,
    )
    gu_t = w_gate_up[0].reshape(part, 2 * tp * 2 * ff_rows).T.reshape(2, tp, 2, ff_rows, part)
    ffn_pack = jnp.concatenate(
        [gu_t.transpose(1, 2, 0, 3, 4).reshape(tp, 2, 2 * ff_rows, part), w_down[0].reshape(tp, 2, ff_rows, part)],
        axis=2,
    )

    def layers_of(pack):
        mine = lax.dynamic_index_in_dim(pack, c, 1, keepdims=False)
        theirs = at.swap(lax.dynamic_index_in_dim(pack, 1 - c, 1, keepdims=False))
        return jnp.where(first_core, mine, theirs), jnp.where(first_core, theirs, mine)

    attn_layers = layers_of(attn_pack)
    ffn_layers = layers_of(ffn_pack)

    norm_flat = jnp.concatenate([norm_gains[0], norm_shifts[0]], axis=0)
    norm_all = at.all_dp(norm_flat)
    norm_mine = norm_all.transpose(1, 0, 2).reshape(4, width)
    norm_theirs = at.swap(norm_mine)
    norm_layers = [
        jnp.where(first_core, norm_mine, norm_theirs).astype(f32),
        jnp.where(first_core, norm_theirs, norm_mine).astype(f32),
    ]
    bias_all = at.all_dp(b_qkv[0].reshape(3 * heads_j, head_dim // nd))
    bias_mine = bias_all.transpose(1, 0, 2).reshape(3, heads_j, head_dim)
    bias_theirs = at.swap(bias_mine)
    bias_both = jnp.stack(
        [jnp.where(first_core, bias_mine, bias_theirs), jnp.where(first_core, bias_theirs, bias_mine)]
    )
    bias_pieces = [
        lax.dynamic_slice_in_dim(b, (2 * lo + c) * per, per, 2)
        for b in [bias_both] + [at.t_xor(bias_both, e) for e in range(1, nt)]
    ]
    bias_both = jnp.stack(bias_pieces, axis=2).astype(f32).reshape(2, 1, 3 * heads * head_dim)

    order = at.e_order()
    row = jnp.arange(rows_local, dtype=jnp.int32)
    places = jnp.concatenate([(lo ^ e) * rows_local + row for e in order])
    tables = [slot_tables(pick(lengths, c ^ f), places, heads, head_dim) for f in range(2)]
    own_valid = tables[0][0][:rows_local, None]

    def split_attn(pieces):
        qkv = jnp.concatenate(
            [piece[t * head_rows : (t + 1) * head_rows] for t in range(3) for piece in pieces], axis=0
        )
        out = jnp.concatenate([piece[3 * head_rows :] for piece in pieces], axis=0)
        return qkv, out

    def split_ffn(pieces):
        return tuple(
            jnp.concatenate([piece[t * ff_rows : (t + 1) * ff_rows] for piece in pieces], axis=0) for t in range(3)
        )

    pieces = []
    last = None
    for layer in range(2):
        for pack in (attn_layers[layer], ffn_layers[layer]):
            if last is not None:
                pack = after(pack, last)
            got = at.weights_in(pack)
            last = got[0]
            pieces.append(got)
    attn_weights = [split_attn(pieces[0]), split_attn(pieces[2])]
    ffn_weights = [split_ffn(pieces[1]), split_ffn(pieces[3])]

    def forward(layer, rows):
        w_q, w_o = attn_weights[layer]
        w_g, w_u, w_d = ffn_weights[layer]
        norm = norm_layers[layer]
        bias = bias_both[layer]
        normed, unit_one, inverse_one = norm_forward(rows, norm[0], norm[2])
        one = at.gather_rows(normed)
        attended, kept_heads, partial = [], [], []
        for f in range(2):
            projected = dot_nt(one[f], w_q) + bias
            a, k = attend(projected, tables[f][2], tables[f][1], heads, score_scale)
            attended.append(a)
            kept_heads.append(k)
            partial.append(dot_nn(a, w_o))
        middle = rows + at.scatter_rows(partial[0], partial[1].astype(bf16))
        normed, unit_two, inverse_two = norm_forward(middle, norm[1], norm[3])
        two = at.gather_rows(normed)
        gates, ups, hiddens, partial = [], [], [], []
        for f in range(2):
            gate = dot_nt(two[f], w_g)
            up = dot_nt(two[f], w_u)
            hidden = (jax.nn.silu(gate) * up).astype(bf16)
            gates.append(gate)
            ups.append(up)
            hiddens.append(hidden)
            partial.append(dot_nn(hidden, w_d))
        out = (middle + at.scatter_rows(partial[0], partial[1].astype(bf16))) * own_valid
        kept = (unit_one, inverse_one, one, kept_heads, attended, unit_two, inverse_two, two, gates, ups, hiddens)
        return out.astype(bf16), kept

    def backward(layer, grad, kept):
        w_q, w_o = attn_weights[layer]
        w_g, w_u, w_d = ffn_weights[layer]
        norm = norm_layers[layer]
        unit_one, inverse_one, one, kept_heads, attended, unit_two, inverse_two, two, gates, ups, hiddens = kept
        grad = grad * own_valid
        branch = at.gather_rows(grad.astype(bf16))
        grad_gates, grad_ups, partial = [], [], []
        for f in range(2):
            grad_hidden = dot_nt(branch[f], w_d)
            sig = jax.nn.sigmoid(gates[f])
            grad_gate = (grad_hidden * ups[f] * sig * (1.0 + gates[f] * (1.0 - sig))).astype(bf16)
            grad_up = (grad_hidden * gates[f] * sig).astype(bf16)
            grad_gates.append(grad_gate)
            grad_ups.append(grad_up)
            partial.append(dot_nn(grad_gate, w_g) + dot_nn(grad_up, w_u))
        grad_two = at.scatter_rows(partial[0], partial[1].astype(bf16))
        branch_all = jnp.concatenate(branch, axis=0)
        two_all = jnp.concatenate(two, axis=0)
        d_down = dot_tn(jnp.concatenate(hiddens, axis=0), branch_all).astype(bf16)
        d_gate = dot_tn(jnp.concatenate(grad_gates, axis=0), two_all).astype(bf16)
        d_up = dot_tn(jnp.concatenate(grad_ups, axis=0), two_all).astype(bf16)
        d_ffn = [
            jnp.concatenate([d[e * ff_rows : (e + 1) * ff_rows] for d in (d_gate, d_up, d_down)], axis=0)
            for e in range(nt)
        ]
        d_ffn = at.grads_out(d_ffn)
        grad_norm, gain_two, shift_two = norm_backward(grad_two, unit_two, inverse_two, norm[1])
        grad_middle = grad + grad_norm
        attn_grad = at.gather_rows(grad_middle.astype(bf16))
        grad_projected, partial = [], []
        for f in range(2):
            grad_attended = dot_nt(attn_grad[f], w_o).astype(bf16)
            gp = attend_back(grad_attended, kept_heads[f], tables[f][2], tables[f][1], heads, score_scale)
            grad_projected.append(gp)
            partial.append(dot_nn(gp, w_q))
        grad_one = at.scatter_rows(partial[0], partial[1].astype(bf16))
        projected_all = jnp.concatenate(grad_projected, axis=0)
        d_qkv = dot_tn(projected_all, jnp.concatenate(one, axis=0)).astype(bf16)
        d_out = dot_tn(jnp.concatenate(attended, axis=0), jnp.concatenate(attn_grad, axis=0)).astype(bf16)
        span = heads * head_dim
        d_attn = [
            jnp.concatenate(
                [d_qkv[t * span + e * head_rows : t * span + (e + 1) * head_rows] for t in range(3)]
                + [d_out[e * head_rows : (e + 1) * head_rows]],
                axis=0,
            )
            for e in range(nt)
        ]
        d_attn = at.grads_out(d_attn)
        d_bias = jnp.sum(projected_all.astype(f32), axis=0).reshape(3, nt, head_rows)
        grad_norm, gain_one, shift_one = norm_backward(grad_one, unit_one, inverse_one, norm[0])
        grad_in = grad_middle + grad_norm
        d_norm = jnp.stack([gain_one, gain_two, shift_one, shift_two])
        return grad_in.astype(bf16), d_attn, d_ffn, d_bias, d_norm

    passed, kept_first = forward(0, own_tokens.astype(f32))
    final, kept_second = forward(1, passed.astype(f32))
    grad_passed, attn_1, ffn_1, bias_1, norm_1 = backward(1, own_grad.astype(f32), kept_second)
    grad_first, attn_0, ffn_0, bias_0, norm_0 = backward(0, grad_passed.astype(f32), kept_first)

    def sections(early, late):
        mine = jnp.where(first_core, early, late)
        theirs = at.swap(jnp.where(first_core, late, early))
        both = jnp.stack([jnp.where(first_core, mine, theirs), jnp.where(first_core, theirs, mine)])
        return at.turn(both)[None]

    section_outs = sections(passed, final)
    input_grads = sections(grad_first, grad_passed)

    def join(early, late):
        mine = jnp.where(first_core, early, late)
        theirs = at.swap(jnp.where(first_core, late, early))
        halves = [jnp.where(first_core, mine, theirs), jnp.where(first_core, theirs, mine)]
        return jnp.stack(halves, axis=1)

    d_attn = join(attn_0, attn_1)
    d_ffn = join(ffn_0, ffn_1)
    d_qkv = d_attn[:, :, : 3 * head_rows].reshape(tp, 2, 3, head_rows, part).transpose(2, 0, 1, 3, 4)
    d_qkv = d_qkv.reshape(-1, part).T.reshape(1, part, 3, heads_j * head_dim).astype(f32)
    d_out = d_attn[:, :, 3 * head_rows :].reshape(1, heads_j * head_dim, part).astype(f32)
    d_gu = d_ffn[:, :, : 2 * ff_rows].reshape(tp, 2, 2, ff_rows, part).transpose(2, 0, 1, 3, 4)
    d_gu = d_gu.reshape(-1, part).T.reshape(1, part, 2, tp * 2 * ff_rows).astype(f32)
    d_down = d_ffn[:, :, 2 * ff_rows :].reshape(1, tp * 2 * ff_rows, part).astype(f32)

    norm_sum = jnp.where(first_core, norm_0, norm_1) + at.swap(jnp.where(first_core, norm_1, norm_0))
    chunks = norm_sum.reshape(4, nd, part).transpose(1, 0, 2)
    norm_sum = pick(chunks, at.g)
    for s in range(1, nd):
        norm_sum = norm_sum + lax.ppermute(
            pick(chunks, (at.g + s) % nd), "dp", [(i, (i + s) % nd) for i in range(nd)]
        )
    bit = 1
    while bit < nt:
        norm_sum = norm_sum + at.t_xor(norm_sum, bit)
        bit *= 2
    grad_gains = norm_sum[None, :2]
    grad_shifts = norm_sum[None, 2:]

    bias_sum = jnp.stack([bias_0, bias_1])
    total = bias_sum[:, :, 0]
    for e in range(1, nt):
        total = total + at.t_xor(bias_sum[:, :, e], e)
    if at.hi > 1:
        total = lax.psum(total, "dp", axis_index_groups=at.hi_groups())
    mine = jnp.where(first_core, total[0], total[1])
    theirs = at.swap(jnp.where(first_core, total[1], total[0]))
    halves = jnp.stack([jnp.where(first_core, mine, theirs), jnp.where(first_core, theirs, mine)])
    slots = [halves] + [at.lo_shift(halves, s) for s in range(1, tp)]
    stacked = jnp.stack(slots)
    every = jnp.stack([pick(stacked, (lo - k) % tp) for k in range(tp)])
    every = every.reshape(tp * 2, 3, per, head_dim).transpose(1, 0, 2, 3).reshape(3, heads_j, head_dim)
    share = head_dim // nd
    grad_bias = lax.dynamic_slice_in_dim(every, at.g * share, share, 2)[None]

    return (section_outs, input_grads, grad_gains, grad_shifts, d_qkv, grad_bias, d_out, d_gu, d_down)


def solution(mesh):
    placed = (
        P(None, ("dp", "tensor"), None),
        P(None, ("dp", "tensor"), None),
        P(None, "dp", None),
        P("pipe", None, "dp"),
        P("pipe", None, "dp"),
        P("pipe", "dp", None, "tensor"),
        P("pipe", None, "tensor", "dp"),
        P("pipe", "tensor", "dp"),
        P("pipe", "dp", None, "tensor"),
        P("pipe", "tensor", "dp"),
    )
    return jax.shard_map(
        on_device,
        mesh=mesh,
        in_specs=placed,
        out_specs=(
            P("pipe", None, ("dp", "tensor"), None),
            P("pipe", None, ("dp", "tensor"), None),
            P("pipe", None, "dp"),
            P("pipe", None, "dp"),
            P("pipe", "dp", None, "tensor"),
            P("pipe", None, "tensor", "dp"),
            P("pipe", "tensor", "dp"),
            P("pipe", "dp", None, "tensor"),
            P("pipe", "tensor", "dp"),
        ),
        check_vma=False,
    )
```
